256 devices in a mesh: grp: 8 (over z), dp: 8 (over x, y_lo), tp: 4 (over y_hi, core).
Axes of the slice: x: 4, y: 4 (y_hi: 2, y_lo: 2; y = y_hi * 2 + y_lo), z: 8, core: 2. Of those that a mesh axis runs over, the one named last changes fastest.
Arguments:
- hidden_last: bfloat16 [1024, 5120], P(('grp', 'dp')), may hold values from -6 to 6
- gain: float32 [5120], replicated, may hold values from 0.25 to 1.75
- w_query: bfloat16 [5120, 2560], P('dp', 'tp'), may hold values from -0.078125 to 0.078125
- w_key: bfloat16 [5120, 512], P('dp', 'tp'), may hold values from -0.078125 to 0.078125
- w_value: bfloat16 [5120, 512], P('dp', 'tp'), may hold values from -0.078125 to 0.078125
- w_out: bfloat16 [2560, 5120], P('tp'), may hold values from -0.125 to 0.125
- cache_keys: bfloat16 [1024, 128, 512], P(('grp', 'dp'), None, 'tp'), may hold values from -6 to 6
- cache_values: bfloat16 [1024, 128, 512], P(('grp', 'dp'), None, 'tp'), may hold values from -6 to 6
- cache_lengths: int32 [1024], P(('grp', 'dp')), may hold values from 1 to 128
- reward_vec: float32 [5120], replicated, may hold values from -0.078125 to 0.078125
- response_counts: int32 [1024], P('grp'), may hold values from 4 to 16
- assignment: int32 [1024], P('grp'), may hold values from 0 to 7, as said below
- responses: bfloat16 [1024, 16, 5120], P(('grp', 'dp'), None, 'tp'), may hold values from -6 to 6
- cotangent: bfloat16 [1024, 16, 5120], P(('grp', 'dp'), None, 'tp'), may hold values from -6 to 6
Outputs:
- decoded: bfloat16 [1024, 5120], P(('grp', 'dp'))
- advantage: float32 [1024], P(('grp', 'dp'))
- layer_out: bfloat16 [1024, 16, 5120], P(('grp', 'dp'), None, 'tp')
- grad_query: float32 [5120, 2560], P('dp', 'tp')
- grad_key: float32 [5120, 512], P('dp', 'tp')
- grad_value: float32 [5120, 512], P('dp', 'tp')
The draws below stay inside these ranges and needn't reach their ends.
Inputs may be any that keep to these rules, and one draw needn't show every extreme that they name: `assignment`: within each group, every training shard receives exactly 16 rows, and from the 16 rows of one device at most 4 rows go to one training shard; that most is reached for some shard in every group.
All inputs are finite; a program needn't handle non-finite values.
Results may differ from the reference program's by a relative error of at most 0.025.
Values may be sent and summed in bfloat16 or wider, within the bound.
No kernel may reach another device: no remote copies, remote signals or barrier semaphores. Data moves between devices by JAX's collectives and lax.ppermute only.
A program may use at most 128 MiB of HBM per device.

```python
import jax
import jax.numpy as jnp
from jax import lax

D = 5120
HEADS = 20
KV_HEADS = 4
HEAD_DIM = 128
STEPS = 2
R_DEV = 16
CACHE = 128
MAXRESP = 16
GROUP_ROWS = 128
ROWS = 1024
N_DP = 8
N_TP = 4


def draw_assignment(key, part):
    shards = GROUP_ROWS // R_DEV
    groups = ROWS // GROUP_ROWS
    base = R_DEV // shards

    def one_group(group_key):
        first_key, second_key = jax.random.split(group_key)
        first = jax.random.permutation(first_key, shards)
        second = jnp.roll(first, -1)
        columns = jnp.arange(shards)
        loads = base + 2 * (columns[None, :] == first[:, None]).astype(jnp.int32) - 2 * (columns[None, :] == second[:, None]).astype(jnp.int32)
        ends = jnp.cumsum(loads, axis=1)
        place = jnp.arange(R_DEV)
        target = jnp.sum((place[None, :, None] >= ends[:, None, :]).astype(jnp.int32), axis=2)
        row_keys = jax.random.split(second_key, shards)
        shuffled = jax.vmap(lambda row_key, row: jax.random.permutation(row_key, row))(row_keys, target)
        return shuffled.reshape(-1)
    group_keys = jax.random.split(jax.random.fold_in(key, 11), groups)
    return jax.vmap(one_group)(group_keys).reshape(-1).astype(jnp.int32)


def set_ends(array, rng, low, high):
    longest = array.shape.index(max(array.shape))
    spots = []
    for shift in (0, 1):
        where = [jax.random.randint(jax.random.fold_in(rng, axis), (), 0, length) for axis, length in enumerate(array.shape)]
        where[longest] = (where[longest] + shift) % array.shape[longest]
        spots.append(tuple(where))
    return array.at[spots[0]].set(low).at[spots[1]].set(high)


def levels(own_key, shape, cuts, smallest, largest):
    loudness = 1.0
    for axis_at, shards_of in cuts:
        steps = jax.random.uniform(jax.random.fold_in(jax.random.fold_in(own_key, 6), axis_at), (shards_of,), jnp.float32, smallest / len(cuts), largest / len(cuts))
        loudness = loudness * jnp.repeat(jnp.exp(steps), shape[axis_at] // shards_of).reshape((-1,) + (1,) * (len(shape) - 1 - axis_at))
    return loudness


def noise(rng, shape, width, bound, pieces=(), kind=jnp.bfloat16):
    result = width * jax.random.normal(rng, shape, jnp.float32)
    if pieces:
        result = result * levels(rng, shape, pieces, -0.22, 0.18)
    return jnp.clip(result, -bound, bound).astype(kind)


def setup_inputs(seed: int = 0) -> dict:
    streams_of = jax.random.split(jax.random.key(seed), 15)
    return {
        "hidden_last": noise(streams_of[0], (ROWS, D), 1.0, 6.0, ((0, 64),)),
        "gain": jnp.clip(1.0 + 0.15 * jax.random.normal(streams_of[1], (D,), jnp.float32), 0.25, 1.75),
        "w_query": noise(streams_of[2], (D, HEADS * HEAD_DIM), D ** -0.5, 0.078125, ((0, 8), (1, 4))),
        "w_key": noise(streams_of[3], (D, KV_HEADS * HEAD_DIM), D ** -0.5, 0.078125, ((0, 8), (1, 4))),
        "w_value": noise(streams_of[4], (D, KV_HEADS * HEAD_DIM), D ** -0.5, 0.078125, ((0, 8), (1, 4))),
        "w_out": noise(streams_of[5], (HEADS * HEAD_DIM, D), (HEADS * HEAD_DIM) ** -0.5, 0.125, ((0, 4),)),
        "cache_keys": noise(streams_of[6], (ROWS, CACHE, KV_HEADS * HEAD_DIM), 1.0, 6.0, ((0, 64), (2, 4))),
        "cache_values": noise(streams_of[7], (ROWS, CACHE, KV_HEADS * HEAD_DIM), 1.0, 6.0, ((0, 64), (2, 4))),
        "cache_lengths": set_ends(jax.random.randint(streams_of[8], (ROWS,), 1, CACHE + 1), jax.random.fold_in(streams_of[8], 1), 1, CACHE).astype(jnp.int32),
        "reward_vec": noise(streams_of[9], (D,), D ** -0.5, 0.078125, (), jnp.float32),
        "response_counts": set_ends(jax.random.randint(streams_of[10], (ROWS,), MAXRESP // 4, MAXRESP + 1), jax.random.fold_in(streams_of[10], 1), MAXRESP // 4, MAXRESP).astype(jnp.int32),
        "assignment": draw_assignment(jax.random.fold_in(streams_of[14], 71), 0),
        "responses": noise(streams_of[12], (ROWS, MAXRESP, D), 1.0, 6.0, ((0, 64), (2, 4))),
        "cotangent": noise(streams_of[13], (ROWS, MAXRESP, D), 1.0, 6.0, ((0, 64), (2, 4))),
    }


def norm_rows(values, gain):
    wide = values.astype(jnp.float32)
    meansq = lax.optimization_barrier(jnp.mean(wide * wide, axis=-1, keepdims=True))
    return (wide * lax.rsqrt(meansq + 1e-06) * gain).astype(jnp.bfloat16)

def rounded(values):
    return lax.optimization_barrier(values.astype(jnp.bfloat16)).astype(jnp.float32)

def decode_attend(query, cache_k, cache_v, lengths, new_k, new_v):
    rows_n = query.shape[0]
    slots = cache_k.shape[1]
    kv_n = cache_k.shape[2] // HEAD_DIM
    per_kv = query.shape[1] // cache_k.shape[2]
    scale = 1.0 / HEAD_DIM ** 0.5
    quer = query.reshape(rows_n, kv_n, per_kv, HEAD_DIM).astype(jnp.float32)
    keys_c = cache_k.reshape(rows_n, slots, kv_n, HEAD_DIM).astype(jnp.float32)
    vals_c = cache_v.reshape(rows_n, slots, kv_n, HEAD_DIM).astype(jnp.float32)
    keys_n = new_k.reshape(rows_n, -1, kv_n, HEAD_DIM).astype(jnp.float32)
    vals_n = new_v.reshape(rows_n, -1, kv_n, HEAD_DIM).astype(jnp.float32)
    score_c = jnp.einsum('rkgd,rckd->rkgc', quer, keys_c) * scale
    score_n = jnp.einsum('rkgd,rnkd->rkgn', quer, keys_n) * scale
    live = (jnp.arange(slots, dtype=jnp.int32)[None, :] < lengths[:, None])[:, None, None, :]
    score_c = jnp.where(live, score_c, -1e+30)
    scores = jnp.concatenate([score_c, score_n], axis=-1)
    expo = jnp.exp(scores)
    weights = (expo / lax.optimization_barrier(jnp.sum(expo, axis=-1, keepdims=True))).astype(jnp.bfloat16).astype(jnp.float32)
    context = jnp.einsum('rkgc,rckd->rkgd', weights[..., :slots], vals_c)
    context = context + jnp.einsum('rkgn,rnkd->rkgd', weights[..., slots:], vals_n)
    return context.reshape(rows_n, -1).astype(jnp.bfloat16)

def attend(query, keys, values, counts):
    rows_n = counts.shape[0]
    tokens = query.shape[0]
    length = tokens // rows_n
    kv_n = keys.shape[1] // HEAD_DIM
    per_kv = query.shape[1] // keys.shape[1]
    scale = 1.0 / HEAD_DIM ** 0.5
    quer = query.reshape(rows_n, length, kv_n, per_kv, HEAD_DIM).astype(jnp.float32)
    keyf = keys.reshape(rows_n, length, kv_n, HEAD_DIM).astype(jnp.float32)
    valf = values.reshape(rows_n, length, kv_n, HEAD_DIM).astype(jnp.float32)
    scores = jnp.einsum('rikgd,rjkd->rkgij', quer, keyf) * scale
    slot = jnp.arange(length, dtype=jnp.int32)
    causal = (slot[None, :] <= slot[:, None])[None, :, :]
    inside = slot[None, None, :] < counts[:, None, None]
    mask = (causal & inside)[:, None, None, :, :]
    scores = jnp.where(mask, scores, -1e+30)
    expo = jnp.exp(scores)
    weights = (expo / lax.optimization_barrier(jnp.sum(expo, axis=-1, keepdims=True))).astype(jnp.bfloat16).astype(jnp.float32)
    context = jnp.einsum('rkgij,rjkd->rikgd', weights, valf)
    return context.reshape(tokens, -1).astype(jnp.bfloat16)

def slot_valid(counts, length):
    slot = jnp.arange(length, dtype=jnp.int32)
    return (slot[None, :] < counts[:, None]).reshape(-1)

def reference(hidden_last, gain, w_query, w_key, w_value, w_out, cache_keys, cache_values, cache_lengths, reward_vec, response_counts, assignment, responses, cotangent):
    state = hidden_last
    keys_new = []
    values_new = []
    for step in range(STEPS):
        normed = norm_rows(state, gain)
        query = jnp.dot(normed, w_query, preferred_element_type=jnp.float32).astype(jnp.bfloat16)
        keys_new.append(jnp.dot(normed, w_key, preferred_element_type=jnp.float32).astype(jnp.bfloat16))
        values_new.append(jnp.dot(normed, w_value, preferred_element_type=jnp.float32).astype(jnp.bfloat16))
        context = decode_attend(query, cache_keys, cache_values, cache_lengths, jnp.stack(keys_new, 1), jnp.stack(values_new, 1))
        output = jnp.dot(context, w_out, preferred_element_type=jnp.float32)
        state = (state.astype(jnp.float32) + output).astype(jnp.bfloat16)
    reward = lax.optimization_barrier(jnp.sum(state.astype(jnp.float32) * reward_vec, axis=-1))
    grouped = reward.reshape(-1, GROUP_ROWS)
    mean = lax.optimization_barrier(jnp.sum(grouped, axis=1, keepdims=True)) / GROUP_ROWS
    spread = lax.optimization_barrier(jnp.sum(grouped * grouped, axis=1, keepdims=True)) / GROUP_ROWS - mean * mean
    advantage = ((grouped - mean) / jnp.sqrt(spread + 1e-05)).reshape(-1)
    adv_short = advantage.astype(jnp.bfloat16)
    head_cols = HEADS * HEAD_DIM // N_TP
    tokens = R_DEV * MAXRESP

    def shard_step(carry, shard):
        group = shard // N_DP
        index = shard % N_DP
        group_assign = lax.dynamic_slice_in_dim(assignment, (group * GROUP_ROWS).astype(jnp.int32), GROUP_ROWS)
        order = jnp.argsort(group_assign * GROUP_ROWS + jnp.arange(GROUP_ROWS, dtype=jnp.int32), stable=True).astype(jnp.int32)
        chosen = lax.dynamic_slice_in_dim(order, (index * R_DEV).astype(jnp.int32), R_DEV) + (group * GROUP_ROWS).astype(jnp.int32)
        inputs = jnp.take(responses, chosen, axis=0).reshape(tokens, D)
        counts = jnp.take(response_counts, chosen)
        weight_row = jnp.take(adv_short, chosen).astype(jnp.float32)
        upstream_raw = lax.dynamic_slice_in_dim(cotangent, (shard * R_DEV).astype(jnp.int32), R_DEV).reshape(tokens, D)
        normed = norm_rows(inputs, gain)
        query = jnp.dot(normed, w_query, preferred_element_type=jnp.float32).astype(jnp.bfloat16)
        keys = jnp.dot(normed, w_key, preferred_element_type=jnp.float32).astype(jnp.bfloat16)
        values = jnp.dot(normed, w_value, preferred_element_type=jnp.float32).astype(jnp.bfloat16)
        valid = slot_valid(counts, MAXRESP)
        context, pull = jax.vjp(lambda a, b, c: attend(a, b, c, counts), query, keys, values)
        summed = inputs.astype(jnp.float32)
        for piece in range(N_TP):
            part = jnp.dot(context[:, piece * head_cols:(piece + 1) * head_cols], w_out[piece * head_cols:(piece + 1) * head_cols], preferred_element_type=jnp.float32)
            summed = summed + rounded(part)
        layer = summed.astype(jnp.bfloat16)
        token_weight = jnp.repeat(weight_row, MAXRESP) * valid.astype(jnp.float32)
        upstream = (token_weight[:, None] * upstream_raw.astype(jnp.float32)).astype(jnp.bfloat16)
        d_context = lax.dot_general(upstream, w_out, (((1,), (1,)), ((), ())), preferred_element_type=jnp.float32).astype(jnp.bfloat16)
        d_parts = pull(d_context)
        sums = []
        for total, grad_in in zip(carry, d_parts):
            term = lax.dot_general(normed, grad_in, (((0,), (0,)), ((), ())), preferred_element_type=jnp.float32)
            sums.append(total + rounded(term))
        return (tuple(sums), layer.reshape(R_DEV, MAXRESP, D))
    start = (jnp.zeros((D, HEADS * HEAD_DIM), jnp.float32), jnp.zeros((D, KV_HEADS * HEAD_DIM), jnp.float32), jnp.zeros((D, KV_HEADS * HEAD_DIM), jnp.float32))
    grads, layers = lax.scan(shard_step, start, jnp.arange(ROWS // R_DEV, dtype=jnp.int32))
    layer_out = layers.reshape(ROWS, MAXRESP, D)
    return (state, advantage, layer_out, grads[0], grads[1], grads[2])
```

```python
import itertools

import jax
import jax.numpy as jnp
import numpy as np
from jax import lax
from jax.sharding import Mesh
from jax.sharding import PartitionSpec as P

HEAD_DIM = 128
STEPS = 2
SIZES = {"x": 4, "yl": 2, "yh": 2, "core": 2}
DP = ("x", "yl")
BF = jnp.bfloat16
F32 = jnp.float32
CHUNKS = ((0, 512), (512, 896))


def permute(value, axes, move):
    sizes = [SIZES[a] for a in axes]
    pairs = []
    for at in itertools.product(*[range(s) for s in sizes]):
        pairs.append((int(np.ravel_multi_index(at, sizes)), int(np.ravel_multi_index(move(*at), sizes))))
    return lax.ppermute(value, axes, pairs)


def swap(value, axis):
    return lax.ppermute(value, axis, [(0, 1), (1, 0)])


def exchange(blocks, axes):
    return lax.all_to_all(blocks, axes, 0, 0, tiled=True)


def share(value, axes, peers):
    return exchange(jnp.broadcast_to(value[None], (peers, *value.shape)), axes)


def held(values):
    return lax.optimization_barrier(values.astype(BF))


def decode_attend(query, cache_k, cache_v, lengths, new_k, new_v):
    rows_n, slots = cache_k.shape[0], cache_k.shape[1]
    kv_n = cache_k.shape[2] // HEAD_DIM
    per_kv = query.shape[1] // cache_k.shape[2]
    scale = 1.0 / HEAD_DIM**0.5
    quer = query.reshape(rows_n, kv_n, per_kv, HEAD_DIM)
    keys_c = cache_k.reshape(rows_n, slots, kv_n, HEAD_DIM)
    vals_c = cache_v.reshape(rows_n, slots, kv_n, HEAD_DIM)
    keys_n = new_k.reshape(rows_n, -1, kv_n, HEAD_DIM)
    vals_n = new_v.reshape(rows_n, -1, kv_n, HEAD_DIM)
    score_c = jnp.einsum("rkgd,rckd->rkgc", quer, keys_c, preferred_element_type=F32) * scale
    score_n = jnp.einsum("rkgd,rnkd->rkgn", quer, keys_n, preferred_element_type=F32) * scale
    live = (jnp.arange(slots, dtype=jnp.int32)[None, :] < lengths[:, None])[:, None, None, :]
    score_c = jnp.where(live, score_c, -1e30)
    scores = jnp.concatenate([score_c, score_n], axis=-1)
    expo = jnp.exp(scores)
    weights = (expo / jnp.sum(expo, axis=-1, keepdims=True)).astype(BF)
    context = jnp.einsum("rkgc,rckd->rkgd", weights[..., :slots], vals_c, preferred_element_type=F32)
    context = context + jnp.einsum(
        "rkgn,rnkd->rkgd", weights[..., slots:], vals_n, preferred_element_type=F32
    )
    return context.reshape(rows_n, -1).astype(BF)


def attend(query, keys, values, counts):
    rows_n = counts.shape[0]
    tokens = query.shape[0]
    length = tokens // rows_n
    kv_n = keys.shape[1] // HEAD_DIM
    per_kv = query.shape[1] // keys.shape[1]
    scale = 1.0 / HEAD_DIM**0.5
    quer = query.reshape(rows_n, length, kv_n, per_kv, HEAD_DIM).astype(F32)
    keyf = keys.reshape(rows_n, length, kv_n, HEAD_DIM).astype(F32)
    valf = values.reshape(rows_n, length, kv_n, HEAD_DIM).astype(F32)
    scores = jnp.einsum("rikgd,rjkd->rkgij", quer, keyf) * scale
    slot = jnp.arange(length, dtype=jnp.int32)
    causal = (slot[None, :] <= slot[:, None])[None, :, :]
    inside = slot[None, None, :] < counts[:, None, None]
    mask = (causal & inside)[:, None, None, :, :]
    scores = jnp.where(mask, scores, -1e30)
    expo = jnp.exp(scores)
    weights = (expo / jnp.sum(expo, axis=-1, keepdims=True)).astype(BF).astype(F32)
    context = jnp.einsum("rkgij,rjkd->rikgd", weights, valf)
    return context.reshape(tokens, -1).astype(BF)


def exclusive_rank(labels, classes):
    onehot = (labels[:, None] == jnp.arange(classes, dtype=jnp.int32)[None, :]).astype(jnp.int32)
    return jnp.sum((jnp.cumsum(onehot, axis=0) - onehot) * onehot, axis=1)


def on_device(
    hidden_last,
    gain,
    w_query,
    w_key,
    w_value,
    w_out,
    cache_keys,
    cache_values,
    cache_lengths,
    reward_vec,
    response_counts,
    assignment,
    responses,
    cotangent,
):
    ix, il, ih, ic = (lax.axis_index(a) for a in ("x", "yl", "yh", "core"))
    me = ix * 2 + il
    rows_dev, length, width = responses.shape
    shards = 8
    group_rows = assignment.shape[0]
    tokens = rows_dev * length
    block = w_query.shape[0]
    model = gain.shape[0]
    heads_q, heads_k = w_query.shape[1], w_key.shape[1]
    cols = heads_q + 2 * heads_k

    positions = jnp.arange(group_rows, dtype=jnp.int32)
    slot_of = assignment * rows_dev + exclusive_rank(assignment, shards)
    picks = slot_of[None, :] == positions[:, None]

    def in_order(per_row):
        return jnp.sum(jnp.where(picks, per_row[None, :], 0), axis=1)

    source = positions // rows_dev
    piece = (
        (((source >> 2) ^ ih) * 2 + (((source >> 1) & 1) ^ ic)) * 2 + ((source & 1) ^ il)
    ) * rows_dev + positions % rows_dev
    landing = in_order(piece)
    counts_all = in_order(response_counts)
    counts = lax.dynamic_slice_in_dim(counts_all, me * rows_dev, rows_dev)

    flat = responses.reshape(tokens, width)
    first, second = flat[:, :block], flat[:, block:]
    halves = [jnp.where(il == 0, first, second), jnp.where(il == 0, second, first)]
    mine, theirs = [], []
    for k in range(2):
        for j in range(2):
            got = permute(
                halves[j],
                ("x", "yl", "yh", "core"),
                lambda x, l, h, c: (2 * h + c, l ^ j, (x // 2) ^ k, x % 2),
            )
            mine.append(got)
            theirs.append(swap(got, "core"))
    gathered = jnp.stack([mine[0], mine[1], theirs[0], theirs[1], mine[2], mine[3], theirs[2], theirs[3]])
    x_all = jnp.take(gathered.reshape(group_rows, length, block), landing, axis=0)
    x_all = x_all.reshape(group_rows * length, block)

    gain_block = lax.dynamic_slice_in_dim(gain, me * block, block)
    weights = jnp.concatenate([w_query, w_key, w_value], axis=1).astype(F32)
    weights = (weights * gain_block[:, None]).astype(BF)

    state = hidden_last
    keys_new, values_new = [], []
    for step in range(STEPS):
        wide = state.astype(F32)
        inv = lax.rsqrt(jnp.mean(wide * wide, axis=-1, keepdims=True) + 1e-06)
        by_block = jnp.swapaxes(state.reshape(rows_dev, shards, block), 0, 1)
        rows_all = exchange(by_block, DP).reshape(group_rows, block)
        part = jnp.dot(rows_all, weights, preferred_element_type=F32)
        summed = exchange(part.reshape(shards, rows_dev, cols), DP).sum(axis=0) * inv
        summed = summed.astype(BF)
        keys_new.append(summed[:, heads_q : heads_q + heads_k])
        values_new.append(summed[:, heads_q + heads_k :])
        context = decode_attend(
            summed[:, :heads_q],
            cache_keys,
            cache_values,
            cache_lengths,
            jnp.stack(keys_new, 1),
            jnp.stack(values_new, 1),
        )
        out = held(jnp.dot(context, w_out, preferred_element_type=F32))
        out = held(out.astype(F32) + swap(out, "core").astype(F32))
        state = held(wide + (out.astype(F32) + swap(out, "yh").astype(F32)))
    reward = jnp.sum(state.astype(F32) * reward_vec, axis=-1)
    rewards = share(reward, DP, shards).reshape(group_rows)
    mean = jnp.sum(rewards) / group_rows
    spread = jnp.sum(rewards * rewards) / group_rows - mean * mean
    advantage_all = (rewards - mean) / jnp.sqrt(spread + 1e-05)
    advantage = lax.dynamic_slice_in_dim(advantage_all, me * rows_dev, rows_dev)
    adv_short = in_order(advantage_all.astype(BF).astype(F32))

    squares = x_all.astype(F32)
    squares = jnp.sum(squares * squares, axis=-1)
    part = jnp.dot(x_all, weights, preferred_element_type=F32).astype(BF)
    parts = exchange(part.reshape(shards, tokens, cols), DP)
    squares = share(squares.reshape(-1, 128), DP, shards).sum(axis=0).reshape(-1)
    inv_all = lax.rsqrt(squares / model + 1e-06)
    inv = lax.dynamic_slice_in_dim(inv_all, me * tokens, tokens)
    train = (parts.astype(F32).sum(axis=0) * inv[:, None]).astype(BF)
    query = train[:, :heads_q]
    keys = train[:, heads_q : heads_q + heads_k]
    values = train[:, heads_q + heads_k :]
    context, pull = jax.vjp(lambda a, b, c: attend(a, b, c, counts), query, keys, values)

    cot = cotangent.reshape(tokens, width)
    cot_other = swap(cot, "yh")
    by_h = [jnp.where(ih == 0, cot, cot_other), jnp.where(ih == 0, cot_other, cot)]
    pieces = []
    for value in by_h:
        other = swap(value, "core")
        pieces += [jnp.where(ic == 0, value, other), jnp.where(ic == 0, other, value)]
    full_cot = jnp.concatenate(pieces, axis=1)
    slot = jnp.arange(length, dtype=jnp.int32)
    valid = (slot[None, :] < counts[:, None]).reshape(-1)
    d_context = lax.dot_general(
        full_cot, w_out, (((1,), (1,)), ((), ())), preferred_element_type=F32
    )
    d_context = jnp.where(valid[:, None], d_context, 0.0).astype(BF)
    d_train = jnp.concatenate(pull(d_context), axis=1)

    row_scale = jnp.repeat(adv_short, length) * inv_all
    grads = []
    for low, high in CHUNKS:
        d_all = share(d_train[:, low:high], DP, shards).reshape(shards * tokens, high - low)
        d_all = (d_all.astype(F32) * row_scale[:, None]).astype(BF)
        grad = lax.dot_general(x_all, d_all, (((0,), (0,)), ((), ())), preferred_element_type=F32)
        grad = (grad * gain_block[:, None]).astype(BF)
        grad = exchange(grad.reshape(8, block // 8, high - low), "grp")
        grad = grad.astype(F32).sum(axis=0).astype(BF)
        grads.append(share(grad, "grp", 8).reshape(block, high - low))
    grad_all = jnp.concatenate(grads, axis=1).astype(F32)

    out = jnp.dot(context, w_out, preferred_element_type=F32).astype(BF)
    quarter = [out[:, t * width : (t + 1) * width] for t in range(4)]
    send = jnp.stack([jnp.where(ic == 0, quarter[2 * h + 1], quarter[2 * h]) for h in range(2)])
    keep = jnp.stack([jnp.where(ic == 0, quarter[2 * h], quarter[2 * h + 1]) for h in range(2)])
    pair = (keep.astype(F32) + swap(send, "core").astype(F32)).astype(BF)
    got = swap(jnp.where(ih == 0, pair[1], pair[0]), "yh")
    layer = jnp.where(ih == 0, pair[0], pair[1]).astype(F32) + got.astype(F32)
    back = []
    for j in range(2):
        shard = (2 * ih + ic) * 2 + (il ^ j)
        back.append(
            permute(
                lax.dynamic_slice_in_dim(x_all, shard * tokens, tokens),
                ("x", "yl", "yh", "core"),
                lambda x, l, h, c: (2 * h + c, l ^ j, x // 2, x % 2),
            )
        )
    local_in = jnp.concatenate(
        [jnp.where(il == 0, back[0], back[1]), jnp.where(il == 0, back[1], back[0])], axis=1
    )
    layer = (local_in.astype(F32) + layer).astype(BF).reshape(rows_dev, length, width)
    return (
        state,
        advantage,
        layer,
        grad_all[:, :heads_q],
        grad_all[:, heads_q : heads_q + heads_k],
        grad_all[:, heads_q + heads_k :],
    )


def solution(mesh):
    fine = Mesh(
        np.asarray(mesh.devices).reshape(8, 4, 2, 2, 2), ("grp", "x", "yl", "yh", "core")
    )
    rows = ("grp", "x", "yl")
    tp = ("yh", "core")
    return jax.shard_map(
        on_device,
        mesh=fine,
        in_specs=(
            P(rows, None),
            P(),
            P(DP, tp),
            P(DP, tp),
            P(DP, tp),
            P(tp, None),
            P(rows, None, tp),
            P(rows, None, tp),
            P(rows),
            P(),
            P("grp"),
            P("grp"),
            P(rows, None, tp),
            P(rows, None, tp),
        ),
        out_specs=(
            P(rows, None),
            P(rows),
            P(rows, None, tp),
            P(DP, tp),
            P(DP, tp),
            P(DP, tp),
        ),
        check_vma=False,
    )
```
